512 devices in a mesh: pix: 128 (over z_hi, x, y, core), row: 4 (over z_lo).
Axes of the slice: x: 4, y: 4, z: 16 (z_hi: 4, z_lo: 4; z = z_hi * 4 + z_lo), core: 2. Of those that a mesh axis runs over, the one named last changes fastest.
Arguments:
- band_images: bfloat16 [256, 128, 8192], P('pix', 'row'), may hold values from -6 to 6
- pivots: int32 [2, 32], replicated, may hold values from 0 to 1048575, as said below
Outputs:
- residual: bfloat16 [8192, 128, 256], P(('pix', 'row'))
- coefficients: bfloat16 [64, 8192, 128], P(None, ('pix', 'row'))
The draws below stay inside these ranges and needn't reach their ends.
Inputs may be any that keep to these rules, and one draw needn't show every extreme that they name: All 64 pivots lie in different columns, and every group of 32 lines starting at a multiple of 32 holds at least one pivot.
All inputs are finite; a program needn't handle non-finite values.
Results may differ from the reference program's by a relative error of at most 0.001.
Values may be sent and summed in bfloat16 or wider, within the bound.
A program may use at most 192 MiB of HBM per device.

```python
import jax
import jax.numpy as jnp
from jax import lax

B = 256
NPIV = 32
LINE_DEV = 32
LINES = 128
COLS = 8192
N_PIX = 128


def draw_pivots(key, part):
    key_cols, key_group, key_first, key_inner = jax.random.split(jax.random.fold_in(key, 11), 4)
    total = 2 * NPIV
    groups = LINES // LINE_DEV
    columns = jax.random.permutation(key_cols, COLS)[:total].astype(jnp.int32)
    chosen = jax.random.randint(key_group, (total,), 0, groups).astype(jnp.int32)
    chosen = chosen.at[:groups].set(jax.random.permutation(key_first, groups).astype(jnp.int32))
    inner = jax.random.randint(key_inner, (total,), 0, LINE_DEV).astype(jnp.int32)
    line_index = chosen * LINE_DEV + inner
    return (line_index * COLS + columns).reshape(2, NPIV).astype(jnp.int32)


def block_levels(stream_key, shape, cuts, low, largest):
    def one(position, shards_of):
        heights = jax.random.uniform(jax.random.fold_in(jax.random.fold_in(stream_key, 6), position), (shards_of,), jnp.float32, low / len(cuts), largest / len(cuts))
        return jnp.repeat(jnp.exp(heights), shape[position] // shards_of).reshape((-1,) + (1,) * (len(shape) - position - 1))

    level = one(*cuts[0])
    for cut in cuts[1:]:
        level = level * one(*cut)
    return level


def centred(own_key, dims, spread, reach, cuts=(), kind=jnp.bfloat16):
    drawn = jax.random.normal(own_key, dims, jnp.float32) * spread
    if len(cuts) > 0:
        drawn = block_levels(own_key, dims, cuts, -0.22, 0.18) * drawn
    return jnp.clip(drawn, min=-reach, max=reach).astype(kind)


def setup_inputs(seed: int = 0) -> dict:
    key_of = jax.random.split(jax.random.key(seed), 3)
    return {
        "band_images": centred(key_of[0], (B, LINES, COLS), 1.0, 6.0, ((0, 128), (1, 4))),
        "pivots": draw_pivots(jax.random.fold_in(key_of[2], 71), 0),
    }


highest = lax.Precision.HIGHEST

def orthonormal(spectra):
    gram = jnp.dot(spectra, spectra.T, precision=highest)
    factor = jnp.linalg.cholesky(gram)
    return jax.scipy.linalg.solve_triangular(factor, spectra, lower=True)

def project(block, basis):
    count = basis.shape[0] // 2
    first = basis[:count]
    second = basis[count:]
    coef_one = jnp.einsum('clb,kb->kcl', block, first, precision=highest)
    remain = block - jnp.einsum('kcl,kb->clb', coef_one, first, precision=highest)
    coef_two = jnp.einsum('clb,kb->kcl', remain, second, precision=highest)
    remain = remain - jnp.einsum('kcl,kb->clb', coef_two, second, precision=highest)
    return (remain.astype(jnp.bfloat16), jnp.concatenate([coef_one, coef_two], axis=0).astype(jnp.bfloat16))

def reference(band_images, pivots):
    flat_images = band_images.reshape(B, LINES * COLS)
    spectra = jnp.take(flat_images, pivots.reshape(-1), axis=1).T.astype(jnp.float32)
    basis = orthonormal(spectra)
    width = COLS // N_PIX

    def one_group(group):
        start = (group * width).astype(jnp.int32)
        piece = lax.dynamic_slice_in_dim(band_images, start, width, 2)
        block = piece.transpose(2, 1, 0).astype(jnp.float32)
        return project(block, basis)
    remains, coefs = lax.map(one_group, jnp.arange(N_PIX, dtype=jnp.int32))
    residual = remains.reshape(COLS, LINES, B)
    coefficients = coefs.transpose(1, 0, 2, 3).reshape(2 * NPIV, COLS, LINES)
    return (residual, coefficients)
```

```python
import functools

import jax
import jax.numpy as jnp
from jax import lax
from jax.experimental import pallas as pl
from jax.experimental.pallas import tpu as pltpu
from jax.sharding import PartitionSpec as P

MESH = pl.DeviceIdType.MESH
HIGHEST = lax.Precision.HIGHEST
NZ = 16
NQ = 32
NPIV = 64
BANDS = 256
NCH = 8
PER = NQ // NCH
SUB = 16 // NCH


def iota(shape, dim):
    return lax.broadcasted_iota(jnp.int32, shape, dim)


def one(mask, kind=jnp.bfloat16):
    return jnp.where(mask, 1.0, 0.0).astype(kind)


def nn(a, b, precision=None):
    return jnp.dot(a, b, precision=precision, preferred_element_type=jnp.float32)


def nt(a, b, precision=None):
    return lax.dot_general(
        a, b, (((1,), (1,)), ((), ())), precision=precision, preferred_element_type=jnp.float32
    )


def tn(a, b, precision=None):
    return lax.dot_general(
        a, b, (((0,), (0,)), ((), ())), precision=precision, preferred_element_type=jnp.float32
    )


def split(w):
    high = w.astype(jnp.bfloat16)
    return high, (w - high.astype(jnp.float32)).astype(jnp.bfloat16)


def far_order(i):
    half = (i + 1) // 2
    return jnp.where(lax.rem(i, 2) == 1, 8 - half, 8 + half)


def exchange(
    a_ref, piv_ref,
    x_ref, mh_ref, ml_ref, ch_ref, cl_ref,
    sb, p1, tb, stage, perm, ps, pz, pq, rs,
    local_sem, z_send, z_recv, q_send, q_recv, pz_send, pz_recv, pq_send, pq_recv,
):
    pix = lax.axis_index("pix")
    row = lax.axis_index("row")
    q = lax.rem(pix, NQ)
    z_hi = pix // NQ
    z = z_hi * 4 + row
    own_chunk = q // PER

    def z_device(zz):
        return ((zz // 4) * NQ + q, lax.rem(zz, 4))

    def q_device(qq):
        return (z_hi * NQ + qq, row)

    barrier = pltpu.get_barrier_semaphore()

    @pl.loop(1, NZ)
    def _(d):
        pl.semaphore_signal(
            barrier, inc=1, device_id=z_device(lax.rem(z + d, NZ)), device_id_type=MESH
        )

    @pl.loop(1, NQ)
    def _(d):
        pl.semaphore_signal(
            barrier, inc=1, device_id=q_device(lax.rem(q + d, NQ)), device_id_type=MESH
        )

    r64, k256 = iota((64, 256), 0), iota((64, 256), 1)
    pick = one(
        ((r64 >> 3) == ((k256 & 127) >> 4))
        & ((r64 & 3) == ((k256 >> 2) & 3))
        & (((r64 >> 2) & 1) == (k256 >> 7))
    )
    lane = iota((32, 128), 1)
    masks = [one((lane & 3) == s) for s in range(4)]

    def chunk_at(k):
        return lax.rem(own_chunk + 1 + k, NCH)

    def relayout(ck):
        for i in range(SUB):
            for zh in range(4):
                col = pl.multiple_of((zh * 16 + ck * SUB + i) * 128, 128)
                halves = []
                for j in range(2):
                    a = a_ref[j, :, pl.ds(col, 128)]
                    halves.append(jnp.concatenate([a * m for m in masks], axis=0))
                out = nt(pick, jnp.concatenate(halves, axis=1)).astype(jnp.bfloat16)
                for m in range(8):
                    sb[ck, zh * 4 + m % 4, (i * 2 + m // 4) * 8 : (i * 2 + m // 4 + 1) * 8, :] = (
                        out[m * 8 : (m + 1) * 8, :]
                    )

    def send_z(k, ck):
        pltpu.make_async_copy(sb.at[ck, z], p1.at[k, z], local_sem.at[k]).start()

        @pl.loop(0, NZ - 1)
        def _(i):
            zz = lax.rem(z + far_order(i), NZ)
            pltpu.make_async_remote_copy(
                sb.at[ck, zz], p1.at[k, z], z_send.at[0], z_recv.at[k],
                device_id=z_device(zz), device_id_type=MESH,
            ).start()

    relayout(chunk_at(0))

    pivots = jnp.concatenate([piv_ref[0:1, :], piv_ref[1:2, :]], axis=1)
    column = pivots & 8191
    offset = (pivots >> 13) - row * 32
    picked = jnp.zeros((64, NPIV), jnp.float32)

    def pick_columns(t, acc):
        at = pl.multiple_of(t * 512, 512)
        hot = one((iota((512, NPIV), 0) + t * 512) == column)
        both = jnp.concatenate(
            [a_ref[0, :, pl.ds(at, 512)], a_ref[1, :, pl.ds(at, 512)]], axis=0
        )
        return acc + nn(both, hot)

    picked = lax.fori_loop(0, 16, pick_columns, picked)
    line = iota((32, NPIV), 0)
    here = jnp.where(line == offset, 1.0, 0.0)
    own = [
        jnp.sum(picked[j * 32 : (j + 1) * 32, :] * here, axis=0, keepdims=True) for j in range(2)
    ]
    rows8 = iota((8, NPIV), 0)
    tile = jnp.where(rows8 == 0, own[0], jnp.where(rows8 == 1, own[1], 0.0))
    ps[...] = jnp.concatenate([tile, jnp.zeros_like(tile)], axis=1).astype(jnp.bfloat16)

    pl.semaphore_wait(barrier, NZ - 1 + NQ - 1)

    pltpu.make_async_copy(ps, pz.at[z], local_sem.at[NCH]).start()

    @pl.loop(0, NZ - 1)
    def _(i):
        zz = lax.rem(z + far_order(i), NZ)
        pltpu.make_async_remote_copy(
            ps, pz.at[z], pz_send.at[0], pz_recv.at[0],
            device_id=z_device(zz), device_id_type=MESH,
        ).start()

    send_z(0, chunk_at(0))

    @pl.loop(1, NCH)
    def _(k):
        ck = chunk_at(k)
        relayout(ck)
        send_z(k, ck)

    pltpu.make_async_copy(ps, pz.at[z], local_sem.at[NCH]).wait()
    pltpu.make_async_copy(pz.at[0 : NZ - 1], pz.at[0 : NZ - 1], pz_recv.at[0]).wait()
    r8 = iota((8, 128), 0)
    plane = jnp.zeros((8, 128), jnp.float32)
    for zh in range(4):
        part = pz[zh * 4].astype(jnp.float32)
        for zl in range(1, 4):
            part = part + pz[zh * 4 + zl].astype(jnp.float32)
        for j in range(2):
            plane = jnp.where(r8 == zh * 2 + j, part[j : j + 1, :], plane)
    pq[...] = plane.astype(jnp.bfloat16)
    pltpu.make_async_copy(pq, rs.at[q], local_sem.at[NCH]).start()

    @pl.loop(1, NQ)
    def _(d):
        pltpu.make_async_remote_copy(
            pq, rs.at[q], pq_send.at[0], pq_recv.at[0],
            device_id=q_device(lax.rem(q + d, NQ)), device_id_type=MESH,
        ).start()

    for t in range(4):
        n512, k128 = iota((128, 512), 1), iota((128, 512), 0)
        perm[t * 128 : (t + 1) * 128, :] = one(
            ((k128 >> 5) == (n512 >> 7)) & (((n512 >> 5) & 3) == t) & ((k128 & 31) == (n512 & 31))
        )

    pltpu.make_async_copy(pq, rs.at[q], local_sem.at[NCH]).wait()
    pltpu.make_async_copy(rs.at[0 : NQ - 1], rs.at[0 : NQ - 1], pq_recv.at[0]).wait()

    arrived = rs[...].astype(jnp.float32).reshape(BANDS, 128).astype(jnp.bfloat16)
    eye = one(iota((NPIV, 128), 0) == iota((NPIV, 128), 1))
    spectra_in = nt(eye, arrived).astype(jnp.bfloat16)
    b_in, b_own = iota((BANDS, BANDS), 0), iota((BANDS, BANDS), 1)
    same = (((b_in >> 1) & 3) * 64 + (b_in >> 3) * 2 + (b_in & 1)) == b_own
    spectra_own = nn(spectra_in, one(same))
    gram = nt(spectra_in, spectra_in)
    sub, lan = iota((NPIV, 128), 0), iota((NPIV, 128), 1)
    wide = jnp.concatenate([gram, one(sub[:, :NPIV] == lan[:, :NPIV], jnp.float32)], axis=1)

    def eliminate(k, w):
        pivot_row = jnp.sum(jnp.where(sub == k, w, 0.0), axis=0, keepdims=True)
        pivot_col = jnp.sum(jnp.where(lan == k, w, 0.0), axis=1, keepdims=True)
        diag = jnp.sum(jnp.where(lan[:1] == k, pivot_row, 0.0), axis=1, keepdims=True)
        ratio = jnp.where(sub[:, :1] > k, pivot_col, 0.0) / diag
        return w - ratio * pivot_row

    wide = lax.fori_loop(0, NPIV, eliminate, wide)
    diag = jnp.sum(jnp.where(sub == lan, wide, 0.0), axis=1, keepdims=True)
    inverse = wide[:, NPIV:] * lax.rsqrt(diag)
    basis_in = nn(inverse, spectra_in.astype(jnp.float32), HIGHEST)
    basis_own = nn(inverse, spectra_own, HIGHEST)
    cross = nt(basis_own[32:], basis_own[:32], HIGHEST)
    coef = jnp.concatenate(
        [basis_in[:32], basis_in[32:] - nn(cross, basis_in[:32], HIGHEST)], axis=0
    )
    remain = one(same, jnp.float32) - tn(coef, basis_own, HIGHEST)
    mh_ref[...], ml_ref[...] = split(remain)
    ch_ref[...], cl_ref[...] = split(coef)

    @pl.loop(0, NCH)
    def _(k):
        ck = chunk_at(k)
        pltpu.make_async_copy(sb.at[ck, z], p1.at[k, z], local_sem.at[k]).wait()
        pltpu.make_async_copy(p1.at[k, 0 : NZ - 1], p1.at[k, 0 : NZ - 1], z_recv.at[k]).wait()
        for zh in range(4):
            lines = jnp.concatenate([p1[k, zh * 4 + zl] for zl in range(4)], axis=1)
            moved = nn(lines, perm[...])
            for i in range(PER):
                for s in range(4):
                    stage[s, (i * 4 + zh) * 8 : (i * 4 + zh + 1) * 8, :] = (
                        moved[i * 8 : (i + 1) * 8, s * 128 : (s + 1) * 128]
                    )
        for i in range(PER):
            for c4 in range(4):
                for s in range(4):
                    rows = stage[s, pl.ds(i * 32 + c4, 8, stride=4), :]
                    tb[k, i, c4 * 4 + s] = rows.astype(jnp.bfloat16)

        for i in range(PER):
            qq = ck * PER + i

            @pl.when(qq != q)
            def _():
                pltpu.make_async_remote_copy(
                    tb.at[k, i], x_ref.at[:, q], q_send.at[0], q_recv.at[0],
                    device_id=q_device(qq), device_id_type=MESH,
                ).start()

            @pl.when(qq == q)
            def _():
                pltpu.make_async_copy(tb.at[k, i], x_ref.at[:, q], local_sem.at[NCH]).start()

    pltpu.make_async_copy(tb.at[0, 0], x_ref.at[:, q], local_sem.at[NCH]).wait()
    pltpu.make_async_copy(
        x_ref.at[:, 0 : NQ - 1], x_ref.at[:, 0 : NQ - 1], q_recv.at[0]
    ).wait()
    pltpu.make_async_copy(
        x_ref.at[:, 0 : NQ - 1], x_ref.at[:, 0 : NQ - 1], q_send.at[0]
    ).wait()
    pltpu.make_async_copy(p1.at[:, 0 : NZ - 1], p1.at[:, 0 : NZ - 1], z_send.at[0]).wait()
    pltpu.make_async_copy(pz.at[0 : NZ - 1], pz.at[0 : NZ - 1], pz_send.at[0]).wait()
    pltpu.make_async_copy(rs.at[0 : NQ - 1], rs.at[0 : NQ - 1], pq_send.at[0]).wait()


def project(x_ref, mh_ref, ml_ref, ch_ref, cl_ref, r_ref, c_ref):
    for c in range(x_ref.shape[0]):
        x = x_ref[c]
        r_ref[c] = (tn(x, mh_ref[...]) + tn(x, ml_ref[...])).astype(r_ref.dtype)
        c_ref[:, c, :] = (nn(ch_ref[...], x) + nn(cl_ref[...], x)).astype(c_ref.dtype)


def shards(band_images, pivots):
    vmem = pl.BlockSpec(memory_space=pltpu.VMEM)
    half = jnp.bfloat16
    dma = pltpu.SemaphoreType.DMA
    x, mh, ml, ch, cl = pl.pallas_call(
        exchange,
        out_shape=(
            jax.ShapeDtypeStruct((16, NQ, 8, 128), half),
            jax.ShapeDtypeStruct((BANDS, BANDS), half),
            jax.ShapeDtypeStruct((BANDS, BANDS), half),
            jax.ShapeDtypeStruct((NPIV, BANDS), half),
            jax.ShapeDtypeStruct((NPIV, BANDS), half),
        ),
        in_specs=[vmem, vmem],
        out_specs=(vmem,) * 5,
        scratch_shapes=[
            pltpu.VMEM((NCH, NZ, PER * 8, 128), half),
            pltpu.VMEM((NCH, NZ, PER * 8, 128), half),
            pltpu.VMEM((NCH, PER, 16, 8, 128), half),
            pltpu.VMEM((4, PER * 32, 128), jnp.float32),
            pltpu.VMEM((512, 512), half),
            pltpu.VMEM((8, 128), half),
            pltpu.VMEM((NZ, 8, 128), half),
            pltpu.VMEM((8, 128), half),
            pltpu.VMEM((NQ, 8, 128), half),
            dma((NCH + 1,)), dma((1,)), dma((NCH,)), dma((1,)), dma((1,)),
            dma((1,)), dma((1,)), dma((1,)), dma((1,)),
        ],
        compiler_params=pltpu.CompilerParams(
            collective_id=0, has_side_effects=True, vmem_limit_bytes=32 << 20
        ),
        name="exchange",
    )(band_images, pivots)
    whole = lambda *shape: pl.BlockSpec(shape, lambda i: (0,) * len(shape))
    return pl.pallas_call(
        project,
        grid=(2,),
        out_shape=(
            jax.ShapeDtypeStruct((16, 128, BANDS), half),
            jax.ShapeDtypeStruct((NPIV, 16, 128), half),
        ),
        in_specs=[
            pl.BlockSpec((8, BANDS, 128), lambda i: (i, 0, 0)),
            whole(BANDS, BANDS), whole(BANDS, BANDS), whole(NPIV, BANDS), whole(NPIV, BANDS),
        ],
        out_specs=(
            pl.BlockSpec((8, 128, BANDS), lambda i: (i, 0, 0)),
            pl.BlockSpec((NPIV, 8, 128), lambda i: (0, i, 0)),
        ),
        compiler_params=pltpu.CompilerParams(vmem_limit_bytes=24 << 20),
        name="project",
    )(x.reshape(16, BANDS, 128), mh, ml, ch, cl)


def solution(mesh):
    return jax.shard_map(
        shards,
        mesh=mesh,
        in_specs=(P("pix", "row", None), P()),
        out_specs=(P(("pix", "row"), None, None), P(None, ("pix", "row"), None)),
        check_vma=False,
    )
```

```python
import functools

import jax
import jax.numpy as jnp
from jax import lax
from jax.experimental import pallas as pl
from jax.experimental.pallas import tpu as pltpu
from jax.sharding import PartitionSpec as P

MESH = pl.DeviceIdType.MESH
HIGHEST = lax.Precision.HIGHEST
NZ = 16
NQ = 32
NPIV = 64
BANDS = 256
SIZES = (4, 4, 4)
CHIPS = 16 - sum(SIZES)
STARTS = tuple(sum(SIZES[:k]) for k in range(len(SIZES)))
NCH = len(SIZES)


def iota(shape, dim):
    return lax.broadcasted_iota(jnp.int32, shape, dim)


def one(mask, kind=jnp.bfloat16):
    return jnp.where(mask, 1.0, 0.0).astype(kind)


def nn(a, b, precision=None):
    return jnp.dot(a, b, precision=precision, preferred_element_type=jnp.float32)


def nt(a, b, precision=None):
    return lax.dot_general(
        a, b, (((1,), (1,)), ((), ())), precision=precision, preferred_element_type=jnp.float32
    )


def tn(a, b, precision=None):
    return lax.dot_general(
        a, b, (((0,), (0,)), ((), ())), precision=precision, preferred_element_type=jnp.float32
    )


def split(w):
    high = w.astype(jnp.bfloat16)
    return high, (w - high.astype(jnp.float32)).astype(jnp.bfloat16)


def far_order(i):
    half = (i + 1) // 2
    return jnp.where(lax.rem(i, 2) == 1, 8 - half, 8 + half)


def exchange(
    a_hbm, piv_hbm,
    x_ref, mh_ref, ml_ref, ch_ref, cl_ref,
    a_ref, piv_ref, sb, p1, last, crossed, landed, tb, stage, perm, ps, pz, pq, rs,
    in_sem, local_sem, z_send, z_recv, c_send, c_recv, l_send, l_recv, q_send, q_recv, pz_send, pz_recv, pq_send, pq_recv,
):
    pix = lax.axis_index("pix")
    row = lax.axis_index("row")
    q = lax.rem(pix, NQ)
    z_hi = pix // NQ
    z = z_hi * 4 + row
    own_chip = q // 2

    def z_device(zz):
        return ((zz // 4) * NQ + q, lax.rem(zz, 4))

    def q_device(qq):
        return (z_hi * NQ + qq, row)

    load_a = pltpu.make_async_copy(a_hbm, a_ref, in_sem.at[0])
    load_a.start()
    load_piv = pltpu.make_async_copy(piv_hbm, piv_ref, in_sem.at[1])
    load_piv.start()
    barrier = pltpu.get_barrier_semaphore()

    @pl.loop(1, NZ)
    def _(d):
        pl.semaphore_signal(
            barrier, inc=1, device_id=z_device(lax.rem(z + d, NZ)), device_id_type=MESH
        )

    @pl.loop(1, NQ)
    def _(d):
        pl.semaphore_signal(
            barrier, inc=1, device_id=q_device(lax.rem(q + d, NQ)), device_id_type=MESH
        )

    r64, k256 = iota((64, 256), 0), iota((64, 256), 1)
    pick = one(
        ((r64 >> 3) == ((k256 & 127) >> 4))
        & ((r64 & 3) == ((k256 >> 2) & 3))
        & (((r64 >> 2) & 1) == (k256 >> 7))
    )
    lane = iota((32, 128), 1)
    masks = [one((lane & 3) == s) for s in range(4)]

    def chip_at(r):
        return lax.rem(own_chip + 1 + r, 16)

    def tiles(r, store):
        chip = chip_at(r)
        for zh in range(4):
            col = pl.multiple_of((zh * 16 + chip) * 128, 128)
            halves = []
            for j in range(2):
                a = a_ref[j, :, pl.ds(col, 128)]
                halves.append(jnp.concatenate([a * m for m in masks], axis=0))
            out = nt(pick, jnp.concatenate(halves, axis=1)).astype(jnp.bfloat16)
            for m in range(8):
                store(zh * 4 + m % 4, m // 4, out[m * 8 : (m + 1) * 8, :])

    def relayout(k):
        @pl.loop(STARTS[k], STARTS[k] + SIZES[k])
        def _(r):
            def store(zz, core, tile):
                sb[zz, r, core * 8 : (core + 1) * 8, :] = tile

            tiles(r, store)

    def relayout_last():
        @pl.loop(0, CHIPS)
        def _(r):
            def store(zz, core, tile):
                last[r, core, zz] = tile

            tiles(r + 16 - CHIPS, store)

    def cross():
        for r in range(CHIPS):
            for core in range(2):
                qq = chip_at(r + 16 - CHIPS) * 2 + core
                slot = r * 2 + lax.rem(q, 2)

                @pl.when(qq != q)
                def _():
                    pltpu.make_async_remote_copy(
                        last.at[r, core], crossed.at[slot], c_send.at[0], c_recv.at[0],
                        device_id=q_device(qq), device_id_type=MESH,
                    ).start()

                @pl.when(qq == q)
                def _():
                    pltpu.make_async_copy(
                        last.at[r, core], crossed.at[slot], local_sem.at[NCH + 1]
                    ).start()

    def send_last():
        pltpu.make_async_copy(last.at[0, 0], crossed.at[0], local_sem.at[NCH + 1]).wait()
        others = 2 * CHIPS - 1
        pltpu.make_async_copy(
            crossed.at[0:others], crossed.at[0:others], c_recv.at[0]
        ).wait()
        pltpu.make_async_copy(crossed.at[:, z], landed.at[z], local_sem.at[NCH + 1]).start()

        @pl.loop(0, NZ - 1)
        def _(i):
            zz = lax.rem(z + far_order(i), NZ)
            pltpu.make_async_remote_copy(
                crossed.at[:, zz], landed.at[z], l_send.at[0], l_recv.at[0],
                device_id=z_device(zz), device_id_type=MESH,
            ).start()

    def send_z(k):
        part = pl.ds(STARTS[k], SIZES[k])
        pltpu.make_async_copy(sb.at[z, part], p1.at[z, part], local_sem.at[k]).start()

        @pl.loop(0, NZ - 1)
        def _(i):
            zz = lax.rem(z + far_order(i), NZ)
            pltpu.make_async_remote_copy(
                sb.at[zz, part], p1.at[z, part], z_send.at[0], z_recv.at[k],
                device_id=z_device(zz), device_id_type=MESH,
            ).start()

    load_a.wait()
    relayout(0)
    pl.semaphore_wait(barrier, NZ - 1 + NQ - 1)
    send_z(0)

    load_piv.wait()
    pivots = jnp.concatenate([piv_ref[0:1, :], piv_ref[1:2, :]], axis=1)
    column = pivots & 8191
    offset = (pivots >> 13) - row * 32
    picked = jnp.zeros((64, NPIV), jnp.float32)

    def pick_columns(t, acc):
        at = pl.multiple_of(t * 512, 512)
        hot = one((iota((512, NPIV), 0) + t * 512) == column)
        both = jnp.concatenate(
            [a_ref[0, :, pl.ds(at, 512)], a_ref[1, :, pl.ds(at, 512)]], axis=0
        )
        return acc + nn(both, hot)

    picked = lax.fori_loop(0, 16, pick_columns, picked)
    line = iota((32, NPIV), 0)
    here = jnp.where(line == offset, 1.0, 0.0)
    own = [
        jnp.sum(picked[j * 32 : (j + 1) * 32, :] * here, axis=0, keepdims=True) for j in range(2)
    ]
    rows8 = iota((8, NPIV), 0)
    tile = jnp.where(rows8 == 0, own[0], jnp.where(rows8 == 1, own[1], 0.0))
    ps[...] = jnp.concatenate([tile, jnp.zeros_like(tile)], axis=1).astype(jnp.bfloat16)

    pltpu.make_async_copy(ps, pz.at[z], local_sem.at[NCH]).start()

    @pl.loop(0, NZ - 1)
    def _(i):
        zz = lax.rem(z + far_order(i), NZ)
        pltpu.make_async_remote_copy(
            ps, pz.at[z], pz_send.at[0], pz_recv.at[0],
            device_id=z_device(zz), device_id_type=MESH,
        ).start()


    relayout_last()
    cross()
    for k in range(1, NCH):
        relayout(k)
        send_z(k)
    send_last()

    pltpu.make_async_copy(ps, pz.at[z], local_sem.at[NCH]).wait()
    pltpu.make_async_copy(pz.at[0 : NZ - 1], pz.at[0 : NZ - 1], pz_recv.at[0]).wait()
    r8 = iota((8, 128), 0)
    plane = jnp.zeros((8, 128), jnp.float32)
    for zh in range(4):
        part = pz[zh * 4].astype(jnp.float32)
        for zl in range(1, 4):
            part = part + pz[zh * 4 + zl].astype(jnp.float32)
        for j in range(2):
            plane = jnp.where(r8 == zh * 2 + j, part[j : j + 1, :], plane)
    pq[...] = plane.astype(jnp.bfloat16)
    pltpu.make_async_copy(pq, rs.at[q], local_sem.at[NCH]).start()

    @pl.loop(1, NQ)
    def _(d):
        pltpu.make_async_remote_copy(
            pq, rs.at[q], pq_send.at[0], pq_recv.at[0],
            device_id=q_device(lax.rem(q + d, NQ)), device_id_type=MESH,
        ).start()

    for t in range(4):
        n512, k128 = iota((128, 512), 1), iota((128, 512), 0)
        perm[t * 128 : (t + 1) * 128, :] = one(
            ((k128 >> 5) == (n512 >> 7)) & (((n512 >> 5) & 3) == t) & ((k128 & 31) == (n512 & 31))
        )

    pltpu.make_async_copy(pq, rs.at[q], local_sem.at[NCH]).wait()
    pltpu.make_async_copy(rs.at[0 : NQ - 1], rs.at[0 : NQ - 1], pq_recv.at[0]).wait()

    arrived = rs[...].astype(jnp.float32).reshape(BANDS, 128).astype(jnp.bfloat16)
    eye = one(iota((NPIV, 128), 0) == iota((NPIV, 128), 1))
    spectra_in = nt(eye, arrived).astype(jnp.bfloat16)
    b_in, b_own = iota((BANDS, BANDS), 0), iota((BANDS, BANDS), 1)
    same = (((b_in >> 1) & 3) * 64 + (b_in >> 3) * 2 + (b_in & 1)) == b_own
    spectra_own = nn(spectra_in, one(same))
    gram = nt(spectra_in, spectra_in)
    sub, lan = iota((NPIV, 128), 0), iota((NPIV, 128), 1)
    wide = jnp.concatenate([gram, one(sub[:, :NPIV] == lan[:, :NPIV], jnp.float32)], axis=1)

    def eliminate(k, w):
        pivot_row = jnp.sum(jnp.where(sub == k, w, 0.0), axis=0, keepdims=True)
        pivot_col = jnp.sum(jnp.where(lan == k, w, 0.0), axis=1, keepdims=True)
        diag = jnp.sum(jnp.where(lan[:1] == k, pivot_row, 0.0), axis=1, keepdims=True)
        ratio = jnp.where(sub[:, :1] > k, pivot_col, 0.0) / diag
        return w - ratio * pivot_row

    wide = lax.fori_loop(0, NPIV, eliminate, wide)
    diag = jnp.sum(jnp.where(sub == lan, wide, 0.0), axis=1, keepdims=True)
    inverse = wide[:, NPIV:] * lax.rsqrt(diag)
    basis_in = nn(inverse, spectra_in.astype(jnp.float32), HIGHEST)
    basis_own = nn(inverse, spectra_own, HIGHEST)
    cross = nt(basis_own[32:], basis_own[:32], HIGHEST)
    coef = jnp.concatenate(
        [basis_in[:32], basis_in[32:] - nn(cross, basis_in[:32], HIGHEST)], axis=0
    )
    remain = one(same, jnp.float32) - tn(coef, basis_own, HIGHEST)
    mh_ref[...], ml_ref[...] = split(remain)
    ch_ref[...], cl_ref[...] = split(coef)

    def regroup(count, load, store):
        for zh in range(4):
            lines = jnp.concatenate([load(zh * 4 + zl) for zl in range(4)], axis=1)
            moved = nn(lines, perm[...])
            for i in range(count):
                for s in range(4):
                    stage[s, (i * 4 + zh) * 8 : (i * 4 + zh + 1) * 8, :] = (
                        moved[i * 8 : (i + 1) * 8, s * 128 : (s + 1) * 128]
                    )
        for i in range(count):
            for c4 in range(4):
                for s in range(4):
                    rows = stage[s, pl.ds(i * 32 + c4, 8, stride=4), :]
                    store(i, c4 * 4 + s, rows.astype(jnp.bfloat16))

    for k in range(NCH):
        start, size = STARTS[k], SIZES[k]
        part = pl.ds(start, size)
        pltpu.make_async_copy(sb.at[z, part], p1.at[z, part], local_sem.at[k]).wait()
        pltpu.make_async_copy(
            p1.at[0 : NZ - 1, part], p1.at[0 : NZ - 1, part], z_recv.at[k]
        ).wait()

        def load(zz):
            return p1[zz, start : start + size].reshape(size * 16, 128)

        def store(i, c, tile):
            tb[start * 2 + i, c] = tile

        regroup(size * 2, load, store)
        for i in range(size * 2):
            pltpu.make_async_remote_copy(
                tb.at[start * 2 + i], x_ref.at[:, q], q_send.at[0], q_recv.at[0],
                device_id=q_device(chip_at(start + i // 2) * 2 + i % 2), device_id_type=MESH,
            ).start()

    pltpu.make_async_copy(crossed.at[:, z], landed.at[z], local_sem.at[NCH + 1]).wait()
    pltpu.make_async_copy(landed.at[0 : NZ - 1], landed.at[0 : NZ - 1], l_recv.at[0]).wait()
    sources = [
        lax.rem(own_chip + 31 - (r + 16 - CHIPS), 16) * 2 + core
        for r in range(CHIPS) for core in range(2)
    ]

    def load_landed(zz):
        return landed[zz].reshape(CHIPS * 16, 128)

    def store_landed(i, c, tile):
        x_ref[c, sources[i]] = tile

    regroup(CHIPS * 2, load_landed, store_landed)
    far = 2 * sum(SIZES)
    pltpu.make_async_copy(x_ref.at[:, 0:far], x_ref.at[:, 0:far], q_recv.at[0]).wait()
    pltpu.make_async_copy(x_ref.at[:, 0:far], x_ref.at[:, 0:far], q_send.at[0]).wait()
    others = 2 * CHIPS - 1
    pltpu.make_async_copy(crossed.at[0:others], crossed.at[0:others], c_send.at[0]).wait()
    pltpu.make_async_copy(landed.at[0 : NZ - 1], landed.at[0 : NZ - 1], l_send.at[0]).wait()
    pltpu.make_async_copy(p1.at[0 : NZ - 1], p1.at[0 : NZ - 1], z_send.at[0]).wait()
    pltpu.make_async_copy(pz.at[0 : NZ - 1], pz.at[0 : NZ - 1], pz_send.at[0]).wait()
    pltpu.make_async_copy(rs.at[0 : NQ - 1], rs.at[0 : NQ - 1], pq_send.at[0]).wait()


def project(x_ref, mh_ref, ml_ref, ch_ref, cl_ref, r_ref, c_ref):
    for c in range(x_ref.shape[0]):
        x = x_ref[c]
        r_ref[c] = (tn(x, mh_ref[...]) + tn(x, ml_ref[...])).astype(r_ref.dtype)
        c_ref[:, c, :] = (nn(ch_ref[...], x) + nn(cl_ref[...], x)).astype(c_ref.dtype)


def shards(band_images, pivots):
    vmem = pl.BlockSpec(memory_space=pltpu.VMEM)
    half = jnp.bfloat16
    dma = pltpu.SemaphoreType.DMA
    x, mh, ml, ch, cl = pl.pallas_call(
        exchange,
        out_shape=(
            jax.ShapeDtypeStruct((16, NQ, 8, 128), half),
            jax.ShapeDtypeStruct((BANDS, BANDS), half),
            jax.ShapeDtypeStruct((BANDS, BANDS), half),
            jax.ShapeDtypeStruct((NPIV, BANDS), half),
            jax.ShapeDtypeStruct((NPIV, BANDS), half),
        ),
        in_specs=[pl.BlockSpec(memory_space=pltpu.HBM)] * 2,
        out_specs=(vmem,) * 5,
        scratch_shapes=[
            pltpu.VMEM(band_images.shape, half),
            pltpu.VMEM(pivots.shape, jnp.int32),
            pltpu.VMEM((NZ, 16 - CHIPS, 16, 128), half),
            pltpu.VMEM((NZ, 16 - CHIPS, 16, 128), half),
            pltpu.VMEM((CHIPS, 2, NZ, 8, 128), half),
            pltpu.VMEM((2 * CHIPS, NZ, 8, 128), half),
            pltpu.VMEM((NZ, 2 * CHIPS, 8, 128), half),
            pltpu.VMEM((2 * (16 - CHIPS), 16, 8, 128), half),
            pltpu.VMEM((4, max(*SIZES, CHIPS) * 64, 128), jnp.float32),
            pltpu.VMEM((512, 512), half),
            pltpu.VMEM((8, 128), half),
            pltpu.VMEM((NZ, 8, 128), half),
            pltpu.VMEM((8, 128), half),
            pltpu.VMEM((NQ, 8, 128), half),
            dma((2,)), dma((NCH + 2,)), dma((1,)), dma((NCH,)), dma((1,)), dma((1,)),
            dma((1,)), dma((1,)), dma((1,)), dma((1,)),
            dma((1,)), dma((1,)), dma((1,)), dma((1,)),
        ],
        compiler_params=pltpu.CompilerParams(
            collective_id=0, has_side_effects=True, vmem_limit_bytes=32 << 20
        ),
        name="exchange",
    )(
        pltpu.with_memory_space_constraint(band_images, pltpu.HBM),
        pltpu.with_memory_space_constraint(pivots, pltpu.HBM),
    )
    whole = lambda *shape: pl.BlockSpec(shape, lambda i: (0,) * len(shape))
    return pl.pallas_call(
        project,
        grid=(2,),
        out_shape=(
            jax.ShapeDtypeStruct((16, 128, BANDS), half),
            jax.ShapeDtypeStruct((NPIV, 16, 128), half),
        ),
        in_specs=[
            pl.BlockSpec((8, BANDS, 128), lambda i: (i, 0, 0)),
            whole(BANDS, BANDS), whole(BANDS, BANDS), whole(NPIV, BANDS), whole(NPIV, BANDS),
        ],
        out_specs=(
            pl.BlockSpec((8, 128, BANDS), lambda i: (i, 0, 0)),
            pl.BlockSpec((NPIV, 8, 128), lambda i: (0, i, 0)),
        ),
        compiler_params=pltpu.CompilerParams(vmem_limit_bytes=24 << 20),
        name="project",
    )(x.reshape(16, BANDS, 128), mh, ml, ch, cl)


def solution(mesh):
    return jax.shard_map(
        shards,
        mesh=mesh,
        in_specs=(P("pix", "row", None), P()),
        out_specs=(P(("pix", "row"), None, None), P(None, ("pix", "row"), None)),
        check_vma=False,
    )
```

```python
import functools

import jax
import jax.numpy as jnp
from jax import lax
from jax.experimental import pallas as pl
from jax.experimental.pallas import tpu as pltpu
from jax.sharding import PartitionSpec as P

MESH = pl.DeviceIdType.MESH
HIGHEST = lax.Precision.HIGHEST
NZ = 16
NQ = 32
NPIV = 64
BANDS = 256
SIZES = (4, 4, 4)
CHIPS = 16 - sum(SIZES)
STARTS = tuple(sum(SIZES[:k]) for k in range(len(SIZES)))
NCH = len(SIZES)


def iota(shape, dim):
    return lax.broadcasted_iota(jnp.int32, shape, dim)


def one(mask, kind=jnp.bfloat16):
    return jnp.where(mask, 1.0, 0.0).astype(kind)


def nn(a, b, precision=None):
    return jnp.dot(a, b, precision=precision, preferred_element_type=jnp.float32)


def nt(a, b, precision=None):
    return lax.dot_general(
        a, b, (((1,), (1,)), ((), ())), precision=precision, preferred_element_type=jnp.float32
    )


def tn(a, b, precision=None):
    return lax.dot_general(
        a, b, (((0,), (0,)), ((), ())), precision=precision, preferred_element_type=jnp.float32
    )


def split(w):
    high = w.astype(jnp.bfloat16)
    return high, (w - high.astype(jnp.float32)).astype(jnp.bfloat16)


def far_order(i):
    half = (i + 1) // 2
    return jnp.where(lax.rem(i, 2) == lax.rem(lax.axis_index("pix"), 2), 8 - half, 8 + half)


def exchange(
    a_hbm, piv_hbm,
    x_ref, m_ref, c_ref,
    a_ref, piv_ref, sb, p1, last, crossed, landed, tb, stage, perm, ps, pz, pq, rs,
    in_sem, local_sem, z_send, z_recv, c_send, c_recv, l_send, l_recv, q_send, q_recv, pz_send, pz_recv, pq_send, pq_recv,
):
    pix = lax.axis_index("pix")
    row = lax.axis_index("row")
    q = lax.rem(pix, NQ)
    z_hi = pix // NQ
    z = z_hi * 4 + row
    own_chip = q // 2

    def z_device(zz):
        return ((zz // 4) * NQ + q, lax.rem(zz, 4))

    def q_device(qq):
        return (z_hi * NQ + qq, row)

    load_a = pltpu.make_async_copy(a_hbm, a_ref, in_sem.at[0])
    load_a.start()
    load_piv = pltpu.make_async_copy(piv_hbm, piv_ref, in_sem.at[1])
    load_piv.start()
    barrier = pltpu.get_barrier_semaphore()

    @pl.loop(1, NZ)
    def _(d):
        pl.semaphore_signal(
            barrier, inc=1, device_id=z_device(lax.rem(z + d, NZ)), device_id_type=MESH
        )

    @pl.loop(1, NQ)
    def _(d):
        pl.semaphore_signal(
            barrier, inc=1, device_id=q_device(lax.rem(q + d, NQ)), device_id_type=MESH
        )

    r64, k256 = iota((64, 256), 0), iota((64, 256), 1)
    pick = one(
        ((r64 >> 3) == ((k256 & 127) >> 4))
        & ((r64 & 3) == ((k256 >> 2) & 3))
        & (((r64 >> 2) & 1) == (k256 >> 7))
    )
    lane = iota((32, 128), 1)
    masks = [one((lane & 3) == s) for s in range(4)]

    def chip_at(r):
        return lax.rem(own_chip + 1 + r, 16)

    def tiles(r, store):
        chip = chip_at(r)
        for zh in range(4):
            col = pl.multiple_of((zh * 16 + chip) * 128, 128)
            halves = []
            for j in range(2):
                a = a_ref[j, :, pl.ds(col, 128)]
                halves.append(jnp.concatenate([a * m for m in masks], axis=0))
            out = nt(pick, jnp.concatenate(halves, axis=1)).astype(jnp.bfloat16)
            for m in range(8):
                store(zh * 4 + m % 4, m // 4, out[m * 8 : (m + 1) * 8, :])

    def relayout(k):
        @pl.loop(STARTS[k], STARTS[k] + SIZES[k])
        def _(r):
            def store(zz, core, tile):
                sb[zz, r, core * 8 : (core + 1) * 8, :] = tile

            tiles(r, store)

    def relayout_last():
        @pl.loop(0, CHIPS)
        def _(r):
            def store(zz, core, tile):
                last[r, core, zz] = tile

            tiles(r + 16 - CHIPS, store)

    def cross():
        for r in range(CHIPS):
            for core in range(2):
                qq = chip_at(r + 16 - CHIPS) * 2 + core
                slot = r * 2 + lax.rem(q, 2)

                @pl.when(qq != q)
                def _():
                    pltpu.make_async_remote_copy(
                        last.at[r, core], crossed.at[:, slot], c_send.at[0], c_recv.at[0],
                        device_id=q_device(qq), device_id_type=MESH,
                    ).start()

                @pl.when(qq == q)
                def _():
                    pltpu.make_async_copy(
                        last.at[r, core], crossed.at[:, slot], local_sem.at[NCH + 1]
                    ).start()

    def send_last():
        pltpu.make_async_copy(last.at[0, 0], crossed.at[:, 0], local_sem.at[NCH + 1]).wait()
        others = 2 * CHIPS - 1
        pltpu.make_async_copy(
            crossed.at[:, 0:others], crossed.at[:, 0:others], c_recv.at[0]
        ).wait()
        pltpu.make_async_copy(crossed.at[z], landed.at[z], local_sem.at[NCH + 1]).start()

        @pl.loop(0, NZ - 1)
        def _(i):
            zz = lax.rem(z + far_order(i), NZ)
            pltpu.make_async_remote_copy(
                crossed.at[zz], landed.at[z], l_send.at[0], l_recv.at[0],
                device_id=z_device(zz), device_id_type=MESH,
            ).start()

    def send_z(k):
        part = pl.ds(STARTS[k], SIZES[k])
        pltpu.make_async_copy(sb.at[z, part], p1.at[z, part], local_sem.at[k]).start()

        @pl.loop(0, NZ - 1)
        def _(i):
            zz = lax.rem(z + far_order(i), NZ)
            pltpu.make_async_remote_copy(
                sb.at[zz, part], p1.at[z, part], z_send.at[0], z_recv.at[k],
                device_id=z_device(zz), device_id_type=MESH,
            ).start()

    load_a.wait()
    relayout(0)
    pl.semaphore_wait(barrier, NZ - 1 + NQ - 1)
    send_z(0)

    load_piv.wait()
    pivots = jnp.concatenate([piv_ref[0:1, :], piv_ref[1:2, :]], axis=1)
    column = pivots & 8191
    offset = (pivots >> 13) - row * 32
    picked = jnp.zeros((64, NPIV), jnp.float32)

    def pick_columns(t, acc):
        at = pl.multiple_of(t * 512, 512)
        hot = one((iota((512, NPIV), 0) + t * 512) == column)
        both = jnp.concatenate(
            [a_ref[0, :, pl.ds(at, 512)], a_ref[1, :, pl.ds(at, 512)]], axis=0
        )
        return acc + nn(both, hot)

    picked = lax.fori_loop(0, 16, pick_columns, picked)
    line = iota((32, NPIV), 0)
    here = jnp.where(line == offset, 1.0, 0.0)
    own = [
        jnp.sum(picked[j * 32 : (j + 1) * 32, :] * here, axis=0, keepdims=True) for j in range(2)
    ]
    rows8 = iota((8, NPIV), 0)
    tile = jnp.where(rows8 == 0, own[0], jnp.where(rows8 == 1, own[1], 0.0))
    ps[...] = jnp.concatenate([tile, jnp.zeros_like(tile)], axis=1).astype(jnp.bfloat16)

    pltpu.make_async_copy(ps, pz.at[z], local_sem.at[NCH]).start()

    @pl.loop(0, NZ - 1)
    def _(i):
        zz = lax.rem(z + far_order(i), NZ)
        pltpu.make_async_remote_copy(
            ps, pz.at[z], pz_send.at[0], pz_recv.at[0],
            device_id=z_device(zz), device_id_type=MESH,
        ).start()


    relayout_last()
    cross()
    for k in range(1, NCH):
        relayout(k)
        send_z(k)
    send_last()

    pltpu.make_async_copy(ps, pz.at[z], local_sem.at[NCH]).wait()
    pltpu.make_async_copy(pz.at[0 : NZ - 1], pz.at[0 : NZ - 1], pz_recv.at[0]).wait()
    r8 = iota((8, 128), 0)
    plane = jnp.zeros((8, 128), jnp.float32)
    for zh in range(4):
        part = pz[zh * 4].astype(jnp.float32)
        for zl in range(1, 4):
            part = part + pz[zh * 4 + zl].astype(jnp.float32)
        for j in range(2):
            plane = jnp.where(r8 == zh * 2 + j, part[j : j + 1, :], plane)
    pq[...] = plane.astype(jnp.bfloat16)
    pltpu.make_async_copy(pq, rs.at[q], local_sem.at[NCH]).start()

    @pl.loop(1, NQ)
    def _(d):
        pltpu.make_async_remote_copy(
            pq, rs.at[q], pq_send.at[0], pq_recv.at[0],
            device_id=q_device(lax.rem(q + d, NQ)), device_id_type=MESH,
        ).start()

    for t in range(4):
        n512, k128 = iota((128, 512), 1), iota((128, 512), 0)
        perm[t * 128 : (t + 1) * 128, :] = one(
            ((k128 >> 5) == (n512 >> 7)) & (((n512 >> 5) & 3) == t) & ((k128 & 31) == (n512 & 31))
        )

    pltpu.make_async_copy(pq, rs.at[q], local_sem.at[NCH]).wait()
    pltpu.make_async_copy(rs.at[0 : NQ - 1], rs.at[0 : NQ - 1], pq_recv.at[0]).wait()

    arrived = rs[...].astype(jnp.float32).reshape(BANDS, 128).astype(jnp.bfloat16)
    eye = one(iota((NPIV, 128), 0) == iota((NPIV, 128), 1))
    spectra_in = nt(eye, arrived).astype(jnp.bfloat16)
    b_in, b_own = iota((BANDS, BANDS), 0), iota((BANDS, BANDS), 1)
    same = (((b_in >> 1) & 3) * 64 + (b_in >> 3) * 2 + (b_in & 1)) == b_own
    spectra_own = nn(spectra_in, one(same))
    gram = nt(spectra_in, spectra_in)
    sub, lan = iota((NPIV, 128), 0), iota((NPIV, 128), 1)
    wide = jnp.concatenate([gram, one(sub[:, :NPIV] == lan[:, :NPIV], jnp.float32)], axis=1)

    def eliminate(k, w):
        pivot_row = jnp.sum(jnp.where(sub == k, w, 0.0), axis=0, keepdims=True)
        pivot_col = jnp.sum(jnp.where(lan == k, w, 0.0), axis=1, keepdims=True)
        diag = jnp.sum(jnp.where(lan[:1] == k, pivot_row, 0.0), axis=1, keepdims=True)
        ratio = jnp.where(sub[:, :1] > k, pivot_col, 0.0) / diag
        return w - ratio * pivot_row

    wide = lax.fori_loop(0, NPIV, eliminate, wide)
    diag = jnp.sum(jnp.where(sub == lan, wide, 0.0), axis=1, keepdims=True)
    inverse = wide[:, NPIV:] * lax.rsqrt(diag)
    basis_in = nn(inverse, spectra_in.astype(jnp.float32), HIGHEST)
    basis_own = nn(inverse, spectra_own, HIGHEST)
    cross = nt(basis_own[32:], basis_own[:32], HIGHEST)
    coef = jnp.concatenate(
        [basis_in[:32], basis_in[32:] - nn(cross, basis_in[:32], HIGHEST)], axis=0
    )
    remain = one(same, jnp.float32) - tn(coef, basis_own, HIGHEST)
    m_ref[:BANDS, :], m_ref[BANDS:, :] = split(remain)
    c_ref[:, :BANDS], c_ref[:, BANDS:] = split(coef)

    def regroup(count, load, store):
        for zh in range(4):
            lines = jnp.concatenate([load(zh * 4 + zl) for zl in range(4)], axis=1)
            moved = nn(lines, perm[...])
            for i in range(count):
                for s in range(4):
                    stage[s, (i * 4 + zh) * 8 : (i * 4 + zh + 1) * 8, :] = (
                        moved[i * 8 : (i + 1) * 8, s * 128 : (s + 1) * 128]
                    )
        for i in range(count):
            for c4 in range(4):
                for s in range(4):
                    rows = stage[s, pl.ds(i * 32 + c4, 8, stride=4), :]
                    store(i, c4 * 4 + s, rows.astype(jnp.bfloat16))

    for k in range(NCH):
        start, size = STARTS[k], SIZES[k]
        part = pl.ds(start, size)
        pltpu.make_async_copy(sb.at[z, part], p1.at[z, part], local_sem.at[k]).wait()
        pltpu.make_async_copy(
            p1.at[0 : NZ - 1, part], p1.at[0 : NZ - 1, part], z_recv.at[k]
        ).wait()

        def load(zz):
            return p1[zz, start : start + size].reshape(size * 16, 128)

        def store(i, c, tile):
            tb[start * 2 + i, c] = tile

        regroup(size * 2, load, store)
        for i in range(size * 2):
            pltpu.make_async_remote_copy(
                tb.at[start * 2 + i], x_ref.at[:, q], q_send.at[0], q_recv.at[0],
                device_id=q_device(chip_at(start + i // 2) * 2 + i % 2), device_id_type=MESH,
            ).start()

    pltpu.make_async_copy(crossed.at[z], landed.at[z], local_sem.at[NCH + 1]).wait()
    pltpu.make_async_copy(landed.at[0 : NZ - 1], landed.at[0 : NZ - 1], l_recv.at[0]).wait()
    sources = [
        lax.rem(own_chip + 31 - (r + 16 - CHIPS), 16) * 2 + core
        for r in range(CHIPS) for core in range(2)
    ]

    def load_landed(zz):
        return landed[zz].reshape(CHIPS * 16, 128)

    def store_landed(i, c, tile):
        x_ref[c, sources[i]] = tile

    regroup(CHIPS * 2, load_landed, store_landed)
    far = 2 * sum(SIZES)
    pltpu.make_async_copy(x_ref.at[:, 0:far], x_ref.at[:, 0:far], q_recv.at[0]).wait()
    pltpu.make_async_copy(x_ref.at[:, 0:far], x_ref.at[:, 0:far], q_send.at[0]).wait()
    others = 2 * CHIPS - 1
    pltpu.make_async_copy(crossed.at[:, 0:others], crossed.at[:, 0:others], c_send.at[0]).wait()
    pltpu.make_async_copy(landed.at[0 : NZ - 1], landed.at[0 : NZ - 1], l_send.at[0]).wait()
    pltpu.make_async_copy(p1.at[0 : NZ - 1], p1.at[0 : NZ - 1], z_send.at[0]).wait()
    pltpu.make_async_copy(pz.at[0 : NZ - 1], pz.at[0 : NZ - 1], pz_send.at[0]).wait()
    pltpu.make_async_copy(rs.at[0 : NQ - 1], rs.at[0 : NQ - 1], pq_send.at[0]).wait()


def project(x_ref, m_ref, w_ref, r_hbm, c_hbm, r_ref, c_ref, wide, sem):
    copies = []
    for c in range(16):
        x = x_ref[c]
        t = x.T
        r_ref[c] = nn(jnp.concatenate([t, t], axis=1), m_ref[...]).astype(r_ref.dtype)
        copies.append(pltpu.make_async_copy(r_ref.at[c], r_hbm.at[c], sem.at[c]))
        copies[-1].start()
        wide[c * NPIV : (c + 1) * NPIV, :] = nn(w_ref[...], jnp.concatenate([x, x], axis=0))
    for k in range(NPIV):
        c_ref[k] = wide[pl.ds(k, 16, stride=NPIV), :].astype(c_ref.dtype)
    copies.append(pltpu.make_async_copy(c_ref, c_hbm, sem.at[16]))
    copies[-1].start()
    for copy in copies:
        copy.wait()


def shards(band_images, pivots):
    vmem = pl.BlockSpec(memory_space=pltpu.VMEM)
    half = jnp.bfloat16
    dma = pltpu.SemaphoreType.DMA
    x, m, w = pl.pallas_call(
        exchange,
        out_shape=(
            jax.ShapeDtypeStruct((16, NQ, 8, 128), half),
            jax.ShapeDtypeStruct((2 * BANDS, BANDS), half),
            jax.ShapeDtypeStruct((NPIV, 2 * BANDS), half),
        ),
        in_specs=[pl.BlockSpec(memory_space=pltpu.HBM)] * 2,
        out_specs=(vmem,) * 3,
        scratch_shapes=[
            pltpu.VMEM(band_images.shape, half),
            pltpu.VMEM(pivots.shape, jnp.int32),
            pltpu.VMEM((NZ, 16 - CHIPS, 16, 128), half),
            pltpu.VMEM((NZ, 16 - CHIPS, 16, 128), half),
            pltpu.VMEM((CHIPS, 2, NZ, 8, 128), half),
            pltpu.VMEM((NZ, 2 * CHIPS, 8, 128), half),
            pltpu.VMEM((NZ, 2 * CHIPS, 8, 128), half),
            pltpu.VMEM((2 * (16 - CHIPS), 16, 8, 128), half),
            pltpu.VMEM((4, max(*SIZES, CHIPS) * 64 + 8, 128), jnp.float32),
            pltpu.VMEM((512, 512), half),
            pltpu.VMEM((8, 128), half),
            pltpu.VMEM((NZ, 8, 128), half),
            pltpu.VMEM((8, 128), half),
            pltpu.VMEM((NQ, 8, 128), half),
            dma((2,)), dma((NCH + 2,)), dma((1,)), dma((NCH,)), dma((1,)), dma((1,)),
            dma((1,)), dma((1,)), dma((1,)), dma((1,)),
            dma((1,)), dma((1,)), dma((1,)), dma((1,)),
        ],
        compiler_params=pltpu.CompilerParams(
            collective_id=0, has_side_effects=True, vmem_limit_bytes=32 << 20
        ),
        name="exchange",
    )(
        pltpu.with_memory_space_constraint(band_images, pltpu.HBM),
        pltpu.with_memory_space_constraint(pivots, pltpu.HBM),
    )
    return pl.pallas_call(
        project,
        out_shape=(
            jax.ShapeDtypeStruct((16, 128, BANDS), half),
            jax.ShapeDtypeStruct((NPIV, 16, 128), half),
        ),
        in_specs=[vmem] * 3,
        out_specs=(pl.BlockSpec(memory_space=pltpu.HBM),) * 2,
        scratch_shapes=[
            pltpu.VMEM((16, 128, BANDS), half),
            pltpu.VMEM((NPIV, 16, 128), half),
            pltpu.VMEM((17 * NPIV, 128), jnp.float32),
            dma((17,)),
        ],
        compiler_params=pltpu.CompilerParams(vmem_limit_bytes=24 << 20),
        name="project",
    )(x.reshape(16, BANDS, 128), m, w)


def solution(mesh):
    return jax.shard_map(
        shards,
        mesh=mesh,
        in_specs=(P("pix", "row", None), P()),
        out_specs=(P(("pix", "row"), None, None), P(None, ("pix", "row"), None)),
        check_vma=False,
    )
```
